32 devices in a mesh: aux: 4 (over y, x), row: 4 (over z), col: 2 (over core).
Axes of the slice: x: 2, y: 2, z: 4, core: 2. Of those that a mesh axis runs over, the one named last changes fastest.
Arguments:
- integrals: bfloat16 [2560, 64, 4096], P('aux', ('row', 'col')), may hold values from -6 to 6
- pair_blocks: int32 [2, 64], P(None, ('row', 'col')), may hold values from -1 to 15, as said below
- occupied: bfloat16 [1024, 64], P('col'), may hold values from -0.75 to 0.75
- metric: bfloat16 [2560, 2560], replicated, as said below
Outputs:
- exchange_k: float32 [1024, 1024], P('row', ('aux', 'col'))
The draws below stay inside these ranges and needn't reach their ends.
Inputs may be any that keep to these rules, and one draw needn't show every extreme that they name: `pair_blocks`: A slot of row group r and column group c (slots (r * number of column groups + c) * 8 onward) is empty (-1 in both entries) or names a row block of r's 4 blocks and a column block of c's 8 blocks; no block pair is named twice; live slots of a group come before its empty ones; every group has 4 or more live slots and some group has all 8 live. `metric`: symmetric.
All inputs are finite; a program needn't handle non-finite values.
Results may differ from the reference program's by a relative error of at most 0.0003.
Values sent between devices are 32-bit elements; how exact they have to be, the bound alone decides.
A program may use at most 256 MiB of HBM per device.

```python
import jax
import jax.numpy as jnp
from jax import lax

NAUX = 2560
NBF = 1024
NOCC = 64
BS = 64
CAP = 8
NRB = 4
NCB = 8
SLOTS = 64
N_ROW = 4
N_COL = 2


def draw_pair_blocks(key, part):
    groups = N_ROW * N_COL
    per_group = NRB * NCB
    key_count, key_forced, key_score = jax.random.split(jax.random.fold_in(key, 11), 3)
    counts = jax.random.randint(key_count, (groups,), max(1, CAP // 2), CAP + 1)
    forced = jax.random.randint(key_forced, (), 0, groups)
    counts = jnp.where(jnp.arange(groups) == forced, CAP, counts)
    scores = jax.random.randint(key_score, (groups, per_group), 0, 1 << 20) * per_group + jnp.arange(per_group)[None, :]
    ranked = jnp.argsort(scores, axis=1)[:, :CAP]
    group_row = jnp.arange(groups) // N_COL
    group_col = jnp.arange(groups) % N_COL
    row_ids = group_row[:, None] * NRB + ranked // NCB
    col_ids = group_col[:, None] * NCB + ranked % NCB
    filled = jnp.arange(CAP)[None, :] < counts[:, None]
    row_ids = jnp.where(filled, row_ids, -1)
    col_ids = jnp.where(filled, col_ids, -1)
    return jnp.stack([row_ids.reshape(-1), col_ids.reshape(-1)]).astype(jnp.int32)


def draw_metric(key, part):
    key_off, key_diag = jax.random.split(jax.random.fold_in(key, 23))
    factor = (NAUX * NOCC) ** (-0.25)
    raw = jax.random.normal(key_off, (NAUX, NAUX), jnp.float32)
    diag = jnp.exp(jax.random.uniform(key_diag, (NAUX,), jnp.float32, -0.7, 0.7))
    sym = (raw + raw.T) * (0.35 / jnp.sqrt(jnp.float32(NAUX)))
    matrix = sym * (1.0 - jnp.eye(NAUX, dtype=jnp.float32)) + jnp.diag(diag)
    return (matrix * factor).astype(jnp.bfloat16)


def steps_of(own_key, extent, cuts, low, top_value):
    loudness, own = 1.0, jax.random.fold_in(own_key, 6)
    for dim, blocks in cuts:
        draws = jnp.exp(jax.random.uniform(jax.random.fold_in(own, dim), (blocks,), jnp.float32, low / len(cuts), top_value / len(cuts)))
        loudness = loudness * jnp.repeat(draws, extent[dim] // blocks).reshape([-1 if axis == dim else 1 for axis in range(len(extent))])
    return loudness


def centred(key, shape, deviation, limit, cuts=(), kind=jnp.bfloat16):
    level = steps_of(key, shape, cuts, -0.22, 0.18) if cuts else 1.0
    entries = jax.random.normal(key, shape, jnp.float32) * deviation * level
    return jnp.minimum(jnp.maximum(entries, -limit), limit).astype(kind)


def setup_inputs(seed: int = 0) -> dict:
    streams_of = jax.random.split(jax.random.key(seed), 5)
    integrals = centred(streams_of[0], (NAUX, SLOTS, BS * BS), 1.0, 6.0, ((0, 4), (1, 8)))
    pair_blocks = draw_pair_blocks(jax.random.fold_in(streams_of[4], 71), 0)
    occupied = centred(streams_of[2], (NBF, NOCC), 0.125, 0.75, ((0, 2),))
    metric = draw_metric(jax.random.fold_in(streams_of[4], 71), 0)
    return dict(integrals=integrals, pair_blocks=pair_blocks, occupied=occupied, metric=metric)


def reference(integrals, pair_blocks, occupied, metric):
    width = min(8, NOCC)
    count = NOCC // width
    zero_index = jnp.zeros((), jnp.int32)
    metric_wide = metric.astype(jnp.float32)

    def one_block(total, index):
        coeffs = lax.dynamic_slice_in_dim(occupied, (index * width).astype(jnp.int32), width, 1).astype(jnp.float32)

        def add_slot(carry, slot):
            row_block = pair_blocks[0, slot]
            col_block = pair_blocks[1, slot]
            filled = (row_block >= 0).astype(jnp.float32)
            safe_row = jnp.maximum(row_block, 0).astype(jnp.int32)
            safe_col = jnp.maximum(col_block, 0).astype(jnp.int32)
            tile = lax.dynamic_index_in_dim(integrals, slot, 1, False).astype(jnp.float32).reshape(NAUX, BS, BS)
            cpart = lax.dynamic_slice_in_dim(coeffs, (safe_col * BS).astype(jnp.int32), BS, 0)
            piece = jnp.einsum('pmn,ni->pmi', tile, cpart, precision=lax.Precision.HIGHEST) * filled
            starts = (zero_index, (safe_row * BS).astype(jnp.int32), zero_index)
            current = lax.dynamic_slice(carry, starts, (NAUX, BS, width))
            carry = lax.dynamic_update_slice(carry, current + piece, starts)
            return carry, None

        start = jnp.zeros((NAUX, NBF, width), jnp.float32)
        half, _ = lax.scan(add_slot, start, jnp.arange(SLOTS, dtype=jnp.int32))
        fitted = jnp.dot(metric_wide, half.reshape(NAUX, NBF * width), precision=lax.Precision.HIGHEST, preferred_element_type=jnp.float32)
        fitted = fitted.reshape(NAUX, NBF, width)
        flat = jnp.transpose(fitted, (1, 0, 2)).reshape(NBF, NAUX * width)
        total = total + jnp.dot(flat, flat.T, precision=lax.Precision.HIGHEST, preferred_element_type=jnp.float32)
        return total, None

    result, _ = lax.scan(one_block, jnp.zeros((NBF, NBF), jnp.float32), jnp.arange(count, dtype=jnp.int32))
    return result
```

```python
import functools

import jax
import jax.numpy as jnp
from jax import lax
from jax.experimental import pallas as pl
from jax.experimental.pallas import tpu as pltpu
from jax.sharding import PartitionSpec as P

BS = 64
OCT = 8
EIGHTHS = (1, 3, 3, 1)
QT = 256
VMEM_LIMIT = 60 * 1024 * 1024


def gathered_plan(integrals, pair_blocks, occupied, metric, nbf):
    aux_rows, slot_count = integrals.shape[:2]
    occ_count = occupied.shape[1]
    rows_local = nbf // lax.axis_size("row")
    row_blocks = rows_local // BS
    metric_wide = metric.astype(jnp.float32)

    def add_slot(carry, slot):
        row_block = pair_blocks[0, slot]
        col_block = pair_blocks[1, slot]
        local_row = jnp.maximum(row_block, 0) % row_blocks
        local_col = jnp.maximum(col_block, 0) % (occupied.shape[0] // BS)
        tile = lax.dynamic_index_in_dim(integrals, slot, 1, False).reshape(aux_rows, BS, BS)
        cpart = lax.dynamic_slice_in_dim(occupied, local_col * BS, BS, 0)
        piece = jnp.einsum("pmn,ni->ipm", tile, cpart, preferred_element_type=jnp.float32)
        piece = jnp.where(row_block >= 0, piece, 0.0)
        current = lax.dynamic_slice_in_dim(carry, local_row * BS, BS, 2)
        return lax.dynamic_update_slice_in_dim(carry, current + piece, local_row * BS, 2), None

    start = jnp.zeros((occ_count, aux_rows, rows_local), jnp.float32)
    partials, _ = lax.scan(add_slot, start, jnp.arange(slot_count, dtype=jnp.int32))
    summed = lax.psum_scatter(partials, "col", scatter_dimension=1, tiled=True)
    half = lax.all_to_all(summed, ("aux", "col"), split_axis=0, concat_axis=1, tiled=True)
    highest = dict(precision=lax.Precision.HIGHEST, preferred_element_type=jnp.float32)
    fitted = jnp.einsum("qp,ipm->iqm", metric_wide, half, **highest)
    contrib = jnp.einsum("iqm,iqn->mn", fitted, lax.all_gather(fitted, "row", axis=2, tiled=True), **highest)
    return lax.psum_scatter(contrib, ("aux", "col"), scatter_dimension=1, tiled=True)


def contract_kernel(rows_ref, w_ref, x_ref, other_ref, mine_ref):
    slots = x_ref.shape[0]
    occ, _, octet, aux_rows = mine_ref.shape
    for h, out_ref in enumerate((other_ref, mine_ref)):
        out_ref[...] = jnp.zeros_like(out_ref)

        def one(s, _):
            w = w_ref[s, h * occ * octet : (h + 1) * occ * octet]
            piece = lax.dot_general(w, x_ref[s], (((1,), (1,)), ((), ())), preferred_element_type=jnp.float32)
            b = rows_ref[s]
            out_ref[:, b] = out_ref[:, b] + piece.reshape(occ, octet, aux_rows)
            return 0

        lax.fori_loop(0, slots, one, 0)


def contract(x, w, rows, row_blocks, occ):
    slots, aux_rows, width = x.shape
    m = width // BS
    out = jax.ShapeDtypeStruct((occ // 2, row_blocks, m, aux_rows), jnp.float32)
    spec = pl.BlockSpec((occ // 2, row_blocks, OCT, aux_rows), lambda j, rows: (0, 0, j, 0))
    return pl.pallas_call(
        contract_kernel,
        grid_spec=pltpu.PrefetchScalarGridSpec(
            num_scalar_prefetch=1,
            grid=(m // OCT,),
            in_specs=[
                pl.BlockSpec(w.shape, lambda j, rows: (0, 0, 0), pipeline_mode=pl.Buffered(1)),
                pl.BlockSpec((slots, aux_rows, OCT * BS), lambda j, rows: (0, 0, j)),
            ],
            out_specs=[spec, spec],
        ),
        out_shape=[out, out],
        compiler_params=pltpu.CompilerParams(vmem_limit_bytes=VMEM_LIMIT),
        cost_estimate=pl.CostEstimate(
            flops=2 * slots * aux_rows * occ * OCT * width,
            bytes_accessed=2 * x.size + 4 * occ * row_blocks * m * aux_rows,
            transcendentals=0,
        ),
        name="contract",
    )(rows, w, x)


def combine_kernel(me_ref, mine_ref, got_ref, *out_refs):
    me = me_ref[0]
    for d, out_ref in enumerate(out_refs):
        dest = lax.bitwise_xor(me, d)
        out_ref[...] = mine_ref[dest] + got_ref[dest]


def combine(me, mine, got):
    group, share, rows, aux_rows = mine.shape
    piece = jax.ShapeDtypeStruct((share, rows, aux_rows), jnp.float32)
    vmem = pl.BlockSpec(memory_space=pltpu.VMEM)
    return pl.pallas_call(
        combine_kernel,
        in_specs=[pl.BlockSpec(memory_space=pltpu.SMEM), vmem, vmem],
        out_specs=[vmem] * group,
        out_shape=[piece] * group,
        compiler_params=pltpu.CompilerParams(vmem_limit_bytes=VMEM_LIMIT),
        cost_estimate=pl.CostEstimate(flops=mine.size, bytes_accessed=12 * mine.size, transcendentals=0),
        name="combine",
    )(me, mine, got)


def high_low(x):
    high = x.astype(jnp.bfloat16)
    return high, (x - high.astype(jnp.float32)).astype(jnp.bfloat16)


def consume_kernel(me_ref, *refs, n_row, starts, sizes, last):
    c = len(sizes) - 1
    refs = list(refs)
    n_pieces = len(refs) - 1 - 2 * c - (1 if c else 0) - (0 if last else 2) - 1 - 2
    pieces, refs = refs[:n_pieces], refs[n_pieces:]
    m_ref, refs = refs[0], refs[1:]
    earlier, refs = refs[: 2 * c], refs[2 * c :]
    if c:
        k_in, refs = refs[0], refs[1:]
    if not last:
        fh_ref, fl_ref, refs = refs[0], refs[1], refs[2:]
    k_ref, hh_ref, hl_ref = refs
    me = me_ref[0]
    share, rows, aux_rows = pieces[0].shape
    total = rows * n_row
    j = pl.program_id(0)

    @pl.when(j == 0)
    def _():
        if c:
            k_ref[...] = k_in[...]
        else:
            k_ref[...] = jnp.zeros_like(k_ref)
        for d, piece in enumerate(pieces):
            source = lax.bitwise_xor(me, d)
            aux = lax.div(source, n_row)
            row = lax.rem(source, n_row)
            lanes = pl.ds(pl.multiple_of(aux * aux_rows, 128), aux_rows)
            for t in range(share):
                high, low = high_low(piece[t])
                at = pl.ds(pl.multiple_of(row * rows, 16) + t * total, rows)
                hh_ref[at, lanes] = high
                hl_ref[at, lanes] = low

    f32 = dict(preferred_element_type=jnp.float32)
    m = m_ref[...]
    fitted = jnp.dot(hh_ref[...], m, **f32) + jnp.dot(hl_ref[...], m, **f32)
    fh, fl = high_low(fitted)
    if not last:
        fh_ref[...] = fh.reshape(fh_ref.shape)
        fl_ref[...] = fl.reshape(fl_ref.shape)

    groups = k_ref.shape[0]
    per = total // groups // sizes[c]

    def outer(a, b):
        return lax.dot_general(a, b, (((1,), (1,)), ((), ())), **f32)

    def add(ci, cj, value):
        at_rows = pl.ds(per * starts[ci], per * sizes[ci])
        at_lanes = pl.ds(groups * per * starts[cj], groups * per * sizes[cj])
        k_ref[:, at_rows, at_lanes] = k_ref[:, at_rows, at_lanes] + value.reshape(
            groups, per * sizes[ci], groups * per * sizes[cj]
        )

    for t in range(share):
        ah, al = fh[t * total : (t + 1) * total], fl[t * total : (t + 1) * total]
        add(c, c, outer(ah, ah) + outer(ah, al) + outer(al, ah))
        for e in range(c):
            bh, bl = earlier[2 * e][t], earlier[2 * e + 1][t]
            add(c, e, outer(ah, bh) + outer(ah, bl) + outer(al, bh))
            add(e, c, outer(bh, ah) + outer(bh, al) + outer(bl, ah))


def consume(me, pieces, metric, earlier, k_so_far, n_row, nbf, groups, starts, sizes, last):
    share, rows, aux_rows = pieces[0].shape
    total = rows * n_row
    n_aux_all = metric.shape[0]
    once = pl.Buffered(1)
    whole = pl.BlockSpec((share, rows, aux_rows), lambda j: (0, 0, 0), pipeline_mode=once)
    in_specs = [pl.BlockSpec(memory_space=pltpu.SMEM)] + [whole] * len(pieces)
    in_specs.append(pl.BlockSpec((n_aux_all, QT), lambda j: (0, j)))
    in_specs += [pl.BlockSpec((f.shape[0], f.shape[1], QT), lambda j: (0, 0, j)) for f in earlier]
    k_shape = (groups, nbf // groups, nbf)
    k_spec = pl.BlockSpec(k_shape, lambda j: (0, 0, 0), pipeline_mode=once)
    args = [me, *pieces, metric, *earlier]
    if k_so_far is not None:
        in_specs.append(k_spec)
        args.append(k_so_far)
    out_specs, out_shape = [], []
    if not last:
        out_specs += [pl.BlockSpec((share, total, QT), lambda j: (0, 0, j))] * 2
        out_shape += [jax.ShapeDtypeStruct((share, total, n_aux_all), jnp.bfloat16)] * 2
    out_specs.append(k_spec)
    out_shape.append(jax.ShapeDtypeStruct(k_shape, jnp.float32))
    scratch = pltpu.VMEM((share * total, n_aux_all), jnp.bfloat16)
    done = groups * (nbf // groups) // BS * sum(sizes)
    return pl.pallas_call(
        functools.partial(consume_kernel, n_row=n_row, starts=starts, sizes=sizes, last=last),
        grid=(n_aux_all // QT,),
        in_specs=in_specs,
        out_specs=out_specs,
        out_shape=out_shape,
        scratch_shapes=[scratch, scratch],
        compiler_params=pltpu.CompilerParams(vmem_limit_bytes=VMEM_LIMIT),
        cost_estimate=pl.CostEstimate(
            flops=4 * share * total * n_aux_all * n_aux_all + 12 * share * total * done * n_aux_all,
            bytes_accessed=2 * metric.size + 4 * share * total * n_aux_all,
            transcendentals=0,
        ),
        name="consume",
    )(*args)


def body(integrals, pair_blocks, occupied, metric, nbf):
    n_aux, n_row, n_col = lax.axis_size("aux"), lax.axis_size("row"), lax.axis_size("col")
    occ = occupied.shape[1]
    devices = n_aux * n_row * n_col
    group = n_aux * n_row
    aux_rows, slots, _ = integrals.shape
    groups = n_aux * n_col
    fits = (
        n_col == 2
        and occ % devices == 0
        and aux_rows % 128 == 0
        and group & (group - 1) == 0
        and nbf % (groups * BS) == 0
        and nbf // BS * OCT % 128 == 0
        and metric.shape[0] % QT == 0
    )
    if not fits:
        return gathered_plan(integrals, pair_blocks, occupied, metric, nbf)
    row_blocks = nbf // n_row // BS
    share = occ // devices
    me = lax.axis_index("aux") * n_row + lax.axis_index("row")
    me_array = me.reshape(1).astype(jnp.int32)

    live = pair_blocks[0] >= 0
    rows = (jnp.maximum(pair_blocks[0], 0) % row_blocks).astype(jnp.int32)
    cols = jnp.maximum(pair_blocks[1], 0) % (occupied.shape[0] // BS)
    swapped = jnp.concatenate([occupied[:, occ // 2 :], occupied[:, : occ // 2]], 1)
    ordered = jnp.where(lax.axis_index("col") == 0, swapped, occupied)
    coeffs = jnp.where(live[:, None, None], ordered.reshape(-1, BS, occ)[cols], 0)
    eye = jnp.eye(OCT, dtype=coeffs.dtype)
    w = (coeffs.transpose(0, 2, 1)[:, :, None, None, :] * eye[None, None, :, :, None]).astype(jnp.bfloat16)
    w = w.reshape(slots, occ * OCT, OCT * BS)

    sizes = tuple(e * BS // 8 for e in EIGHTHS)
    starts = tuple(sum(sizes[:c]) for c in range(len(sizes)))
    arrived = []
    for lo, m in zip(starts, sizes):
        x = jnp.transpose(integrals[:, :, lo * BS : (lo + m) * BS], (1, 0, 2))
        other, mine = contract(x, w, rows, row_blocks, occ)
        got = lax.ppermute(other, "col", [(0, 1), (1, 0)])
        shape = (group, share, row_blocks * m, aux_rows)
        pieces = combine(me_array, mine.reshape(shape), got.reshape(shape))
        sent = [None] * group
        for d in sorted(range(group), key=lambda d: -bin(d).count("1")):
            sent[d] = pieces[d] if d == 0 else lax.ppermute(pieces[d], ("aux", "row"), [(s, s ^ d) for s in range(group)])
        arrived.append(sent)

    earlier, total = [], None
    for c in range(len(sizes)):
        last = c == len(sizes) - 1
        out = consume(
            me_array, arrived[c], metric, earlier, total, n_row, nbf, groups, starts[: c + 1], sizes[: c + 1], last
        )
        total = out[-1]
        earlier += out[:-1]

    part = lax.psum_scatter(total, ("aux", "col"), scatter_dimension=0, tiled=True)[0]
    per = nbf // groups // BS
    blocks = []
    for lo, m in zip(starts, sizes):
        strip = part[:, nbf // BS * lo : nbf // BS * (lo + m)].reshape(-1, nbf // BS, m)
        blocks.append(strip)
    part = jnp.concatenate(blocks, 2)
    part = jnp.concatenate(
        [part[per * lo : per * (lo + m)].reshape(per, m, nbf // BS, BS) for lo, m in zip(starts, sizes)], 1
    )
    part = part.reshape(per * BS, nbf).T
    return lax.psum_scatter(part, "row", scatter_dimension=0, tiled=True)


def solution(mesh):
    def whole(integrals, pair_blocks, occupied, metric):
        nbf = occupied.shape[0]
        return jax.shard_map(
            lambda *args: body(*args, nbf),
            mesh=mesh,
            in_specs=(P("aux", ("row", "col"), None), P(None, ("row", "col")), P("col", None), P()),
            out_specs=P("row", ("aux", "col")),
            check_vma=False,
        )(integrals, pair_blocks, occupied, metric)

    return whole
```

```python
import functools

import jax
import jax.numpy as jnp
from jax import lax
from jax.experimental import pallas as pl
from jax.experimental.pallas import tpu as pltpu
from jax.sharding import PartitionSpec as P

BS = 64
OCT = 8
EIGHTHS = (1, 2, 4, 1)
QT = 512
VMEM_LIMIT = 60 * 1024 * 1024


def gathered_plan(integrals, pair_blocks, occupied, metric, nbf):
    aux_rows, slot_count = integrals.shape[:2]
    occ_count = occupied.shape[1]
    rows_local = nbf // lax.axis_size("row")
    row_blocks = rows_local // BS
    metric_wide = metric.astype(jnp.float32)

    def add_slot(carry, slot):
        row_block = pair_blocks[0, slot]
        col_block = pair_blocks[1, slot]
        local_row = jnp.maximum(row_block, 0) % row_blocks
        local_col = jnp.maximum(col_block, 0) % (occupied.shape[0] // BS)
        tile = lax.dynamic_index_in_dim(integrals, slot, 1, False).reshape(aux_rows, BS, BS)
        cpart = lax.dynamic_slice_in_dim(occupied, local_col * BS, BS, 0)
        piece = jnp.einsum("pmn,ni->ipm", tile, cpart, preferred_element_type=jnp.float32)
        piece = jnp.where(row_block >= 0, piece, 0.0)
        current = lax.dynamic_slice_in_dim(carry, local_row * BS, BS, 2)
        return lax.dynamic_update_slice_in_dim(carry, current + piece, local_row * BS, 2), None

    start = jnp.zeros((occ_count, aux_rows, rows_local), jnp.float32)
    partials, _ = lax.scan(add_slot, start, jnp.arange(slot_count, dtype=jnp.int32))
    summed = lax.psum_scatter(partials, "col", scatter_dimension=1, tiled=True)
    half = lax.all_to_all(summed, ("aux", "col"), split_axis=0, concat_axis=1, tiled=True)
    highest = dict(precision=lax.Precision.HIGHEST, preferred_element_type=jnp.float32)
    fitted = jnp.einsum("qp,ipm->iqm", metric_wide, half, **highest)
    contrib = jnp.einsum("iqm,iqn->mn", fitted, lax.all_gather(fitted, "row", axis=2, tiled=True), **highest)
    return lax.psum_scatter(contrib, ("aux", "col"), scatter_dimension=1, tiled=True)


def contract_kernel(info_ref, occ_ref, x_ref, other_ref, mine_ref, xt_ref, w_ref):
    slots = x_ref.shape[1]
    half, _, octet, aux_rows = mine_ref.shape
    occ = 2 * half
    tall, wide = occ * octet, octet * BS
    f32 = dict(preferred_element_type=jnp.float32)

    @pl.when(pl.program_id(0) == 0)
    def _():
        spread = lax.broadcasted_iota(jnp.int32, (tall, occ), 0) // octet == lax.broadcasted_iota(
            jnp.int32, (tall, occ), 1
        )
        spread = spread.astype(jnp.bfloat16)
        tile = lax.broadcasted_iota(jnp.int32, (BS, wide), 1) % BS == lax.broadcasted_iota(jnp.int32, (BS, wide), 0)
        tile = tile.astype(jnp.bfloat16)
        keep = (
            lax.broadcasted_iota(jnp.int32, (tall, wide), 0) % octet
            == lax.broadcasted_iota(jnp.int32, (tall, wide), 1) // BS
        )

        def build(s, _):
            live = info_ref[1 + 2 * slots + s] > 0
            start = pl.multiple_of(info_ref[1 + slots + s] * BS, BS)
            coeffs = occ_ref[pl.ds(start, BS), :]
            rows = lax.dot_general(spread, coeffs, (((1,), (1,)), ((), ())), **f32).astype(jnp.bfloat16)
            full = jnp.dot(rows, tile, **f32)
            w_ref[s] = jnp.where(jnp.logical_and(keep, live), full, 0.0).astype(jnp.bfloat16)
            return 0

        lax.fori_loop(0, slots, build, 0)

    def turn(q, _):
        at = pl.ds(pl.multiple_of(q * 128, 128), 128)
        xt_ref[:, at] = pltpu.einshape("psk->spk", x_ref[at].astype(jnp.float32)).astype(jnp.bfloat16)
        return 0

    lax.fori_loop(0, aux_rows // 128, turn, 0)
    col = info_ref[0]
    for h, out_ref in ((1 - col, other_ref), (col, mine_ref)):
        out_ref[...] = jnp.zeros_like(out_ref)

        def one(s, _):
            w = w_ref[s, pl.ds(pl.multiple_of(h * half * octet, 16), half * octet)]
            piece = lax.dot_general(w, xt_ref[s], (((1,), (1,)), ((), ())), **f32)
            b = info_ref[1 + s]
            out_ref[:, b] = out_ref[:, b] + piece.reshape(half, octet, aux_rows)
            return 0

        lax.fori_loop(0, slots, one, 0)


def contract(info, occupied, integrals, lo, m, row_blocks):
    aux_rows, slots, _ = integrals.shape
    rows_in, occ = occupied.shape
    out = jax.ShapeDtypeStruct((occ // 2, row_blocks, m, aux_rows), jnp.float32)
    spec = pl.BlockSpec((occ // 2, row_blocks, OCT, aux_rows), lambda j, info: (0, 0, j, 0))
    return pl.pallas_call(
        contract_kernel,
        grid_spec=pltpu.PrefetchScalarGridSpec(
            num_scalar_prefetch=1,
            grid=(m // OCT,),
            in_specs=[
                pl.BlockSpec((rows_in, occ), lambda j, info: (0, 0)),
                pl.BlockSpec((aux_rows, slots, OCT * BS), lambda j, info: (0, 0, j + lo // OCT)),
            ],
            out_specs=[spec, spec],
            scratch_shapes=[
                pltpu.VMEM((slots, aux_rows, OCT * BS), jnp.bfloat16),
                pltpu.VMEM((slots, occ * OCT, OCT * BS), jnp.bfloat16),
            ],
        ),
        out_shape=[out, out],
        compiler_params=pltpu.CompilerParams(vmem_limit_bytes=VMEM_LIMIT),
        cost_estimate=pl.CostEstimate(
            flops=2 * slots * aux_rows * occ * OCT * m * BS,
            bytes_accessed=2 * slots * aux_rows * m * BS + 4 * occ * row_blocks * m * aux_rows,
            transcendentals=0,
        ),
        name="contract",
    )(info, occupied, integrals)


def combine_kernel(me_ref, mine_ref, got_ref, *out_refs):
    me = me_ref[0]
    for d, out_ref in enumerate(out_refs):
        dest = lax.bitwise_xor(me, d)
        out_ref[...] = mine_ref[dest] + got_ref[dest]


def combine(me, mine, got):
    group, share, rows, aux_rows = mine.shape
    piece = jax.ShapeDtypeStruct((share, rows, aux_rows), jnp.float32)
    vmem = pl.BlockSpec(memory_space=pltpu.VMEM)
    return pl.pallas_call(
        combine_kernel,
        in_specs=[pl.BlockSpec(memory_space=pltpu.SMEM), vmem, vmem],
        out_specs=[vmem] * group,
        out_shape=[piece] * group,
        compiler_params=pltpu.CompilerParams(vmem_limit_bytes=VMEM_LIMIT),
        cost_estimate=pl.CostEstimate(flops=mine.size, bytes_accessed=12 * mine.size, transcendentals=0),
        name="combine",
    )(me, mine, got)


def high_low(x):
    high = x.astype(jnp.bfloat16)
    return high, (x - high.astype(jnp.float32)).astype(jnp.bfloat16)


def consume_kernel(me_ref, *refs, n_row, starts, sizes, last):
    c = len(sizes) - 1
    refs = list(refs)
    n_pieces = len(refs) - 4 - 2 * c - (1 if c else 0) - (0 if last else 2)
    pieces, refs = refs[:n_pieces], refs[n_pieces:]
    m_ref, refs = refs[0], refs[1:]
    earlier, refs = refs[: 2 * c], refs[2 * c :]
    if c:
        k_in, refs = refs[0], refs[1:]
    if not last:
        fh_ref, fl_ref, refs = refs[0], refs[1], refs[2:]
    k_ref, h_ref, cross_ref = refs
    me = me_ref[0]
    share, rows, aux_rows = pieces[0].shape
    total = rows * n_row
    blocks = k_ref.shape[0]
    j = pl.program_id(0)

    @pl.when(j == 0)
    def _():
        if c:
            k_ref[...] = k_in[...]
        else:
            k_ref[...] = jnp.zeros_like(k_ref)
        cross_ref[...] = jnp.zeros_like(cross_ref)
        for d, piece in enumerate(pieces):
            source = lax.bitwise_xor(me, d)
            aux = lax.div(source, n_row)
            row = lax.rem(source, n_row)
            lanes = pl.ds(pl.multiple_of(aux * aux_rows, 128), aux_rows)
            for t in range(share):
                high, low = high_low(piece[t])
                at = pl.multiple_of(row * rows, 16)
                h_ref[pl.ds(at + t * total, rows), lanes] = high
                h_ref[pl.ds(at + (share + t) * total, rows), lanes] = low

    f32 = dict(preferred_element_type=jnp.float32)
    both = jnp.dot(h_ref[...], m_ref[...], **f32)
    fh, fl = high_low(both[: share * total] + both[share * total :])
    if not last:
        fh_ref[...] = fh.reshape(fh_ref.shape)
        fl_ref[...] = fl.reshape(fl_ref.shape)

    def outer(a, b):
        a, b = jnp.concatenate(a, 1), jnp.concatenate(b, 1)
        return lax.dot_general(a, b, (((1,), (1,)), ((), ())), **f32)

    def part(ci, cj):
        rows_at = pl.ds(starts[ci], sizes[ci])
        lanes_at = pl.ds(blocks * starts[cj], blocks * sizes[cj])
        return (slice(None), rows_at, lanes_at), (blocks, sizes[ci], blocks * sizes[cj])

    ah = [fh[t * total : (t + 1) * total] for t in range(share)]
    al = [fl[t * total : (t + 1) * total] for t in range(share)]
    at, shape = part(c, c)
    k_ref[at] = k_ref[at] + outer(ah, ah).reshape(shape)
    cross_ref[...] = cross_ref[...] + outer(ah, al)
    for e in range(c):
        bh = [earlier[2 * e][t] for t in range(share)]
        bl = [earlier[2 * e + 1][t] for t in range(share)]
        at, shape = part(c, e)
        k_ref[at] = k_ref[at] + outer(ah + ah + al, bh + bl + bh).reshape(shape)

    @pl.when(j == pl.num_programs(0) - 1)
    def _():
        at, shape = part(c, c)
        cross = cross_ref[...]
        k_ref[at] = k_ref[at] + (cross + cross.T).reshape(shape)
        for e in range(c):
            at, _ = part(c, e)
            turned = k_ref[at].reshape(total, -1).T
            at, shape = part(e, c)
            k_ref[at] = turned.reshape(shape)


def consume(me, pieces, metric, earlier, k_so_far, n_row, nbf, starts, sizes, last):
    share, rows, aux_rows = pieces[0].shape
    total = rows * n_row
    n_aux_all = metric.shape[0]
    once = pl.Buffered(1)
    whole = pl.BlockSpec((share, rows, aux_rows), lambda j: (0, 0, 0), pipeline_mode=once)
    in_specs = [pl.BlockSpec(memory_space=pltpu.SMEM)] + [whole] * len(pieces)
    in_specs.append(pl.BlockSpec((n_aux_all, QT), lambda j: (0, j)))
    in_specs += [pl.BlockSpec((f.shape[0], f.shape[1], QT), lambda j: (0, 0, j)) for f in earlier]
    k_shape = (nbf // BS, BS, nbf)
    k_spec = pl.BlockSpec(k_shape, lambda j: (0, 0, 0), pipeline_mode=once)
    args = [me, *pieces, metric, *earlier]
    if k_so_far is not None:
        in_specs.append(k_spec)
        args.append(k_so_far)
    out_specs, out_shape = [], []
    if not last:
        out_specs += [pl.BlockSpec((share, total, QT), lambda j: (0, 0, j))] * 2
        out_shape += [jax.ShapeDtypeStruct((share, total, n_aux_all), jnp.bfloat16)] * 2
    out_specs.append(k_spec)
    out_shape.append(jax.ShapeDtypeStruct(k_shape, jnp.float32))
    scratch = [pltpu.VMEM((2 * share * total, n_aux_all), jnp.bfloat16), pltpu.VMEM((total, total), jnp.float32)]
    done = nbf // BS * sum(sizes)
    return pl.pallas_call(
        functools.partial(consume_kernel, n_row=n_row, starts=starts, sizes=sizes, last=last),
        grid=(n_aux_all // QT,),
        in_specs=in_specs,
        out_specs=out_specs,
        out_shape=out_shape,
        scratch_shapes=scratch,
        compiler_params=pltpu.CompilerParams(vmem_limit_bytes=VMEM_LIMIT),
        cost_estimate=pl.CostEstimate(
            flops=4 * share * total * n_aux_all * n_aux_all + 6 * share * total * done * n_aux_all,
            bytes_accessed=2 * metric.size + 4 * share * total * n_aux_all,
            transcendentals=0,
        ),
        name="consume",
    )(*args)


def body(integrals, pair_blocks, occupied, metric, nbf):
    n_aux, n_row, n_col = lax.axis_size("aux"), lax.axis_size("row"), lax.axis_size("col")
    occ = occupied.shape[1]
    devices = n_aux * n_row * n_col
    group = n_aux * n_row
    aux_rows, _, _ = integrals.shape
    groups = n_aux * n_col
    fits = (
        n_col == 2
        and occ % devices == 0
        and aux_rows % 128 == 0
        and group & (group - 1) == 0
        and nbf % (groups * BS) == 0
        and nbf // BS * OCT % 128 == 0
        and metric.shape[0] % QT == 0
    )
    if not fits:
        return gathered_plan(integrals, pair_blocks, occupied, metric, nbf)
    row_blocks = nbf // n_row // BS
    share = occ // devices
    me = lax.axis_index("aux") * n_row + lax.axis_index("row")
    me_array = me.reshape(1).astype(jnp.int32)

    live = (pair_blocks[0] >= 0).astype(jnp.int32)
    rows = jnp.maximum(pair_blocks[0], 0) % row_blocks
    cols = jnp.maximum(pair_blocks[1], 0) % (occupied.shape[0] // BS)
    info = jnp.concatenate([lax.axis_index("col").reshape(1).astype(jnp.int32), rows, cols, live]).astype(jnp.int32)

    sizes = tuple(e * BS // 8 for e in EIGHTHS)
    starts = tuple(sum(sizes[:c]) for c in range(len(sizes)))
    arrived = []
    for lo, m in zip(starts, sizes):
        c = len(arrived)
        other, mine = contract(info, occupied, integrals, lo, m, row_blocks)
        got = lax.ppermute(other, "col", [(0, 1), (1, 0)])
        shape = (group, share, row_blocks * m, aux_rows)
        pieces = list(combine(me_array, mine.reshape(shape), got.reshape(shape)))
        info, me_array, pieces[0] = lax.optimization_barrier((info, me_array, pieces[0]))
        sent = [None] * group
        for d in sorted(range(group), key=lambda d: -bin(d).count("1")):
            pairs = [(s, s ^ d) for s in range(group)]
            sent[d] = pieces[d] if d == 0 else lax.ppermute(pieces[d], ("aux", "row"), pairs)
        arrived.append(sent)

    earlier, total = [], None
    for c in range(len(sizes)):
        last = c == len(sizes) - 1
        out = consume(me_array, arrived[c], metric, earlier, total, n_row, nbf, starts[: c + 1], sizes[: c + 1], last)
        total = out[-1]
        earlier += out[:-1]

    blocks = nbf // BS
    part = lax.psum_scatter(total, ("aux", "col"), scatter_dimension=0, tiled=True)
    part = part.reshape(-1, nbf).T
    strips = [part[blocks * lo : blocks * (lo + m)].reshape(blocks, m, -1) for lo, m in zip(starts, sizes)]
    part = jnp.concatenate(strips, 1).reshape(nbf, -1)
    return lax.psum_scatter(part, "row", scatter_dimension=0, tiled=True)


def solution(mesh):
    def local(*args, nbf):
        return body(*args, nbf)

    def whole(integrals, pair_blocks, occupied, metric):
        nbf = occupied.shape[0]
        return jax.shard_map(
            functools.partial(local, nbf=nbf),
            mesh=mesh,
            in_specs=(P("aux", ("row", "col"), None), P(None, ("row", "col")), P("col", None), P()),
            out_specs=P("row", ("aux", "col")),
            check_vma=False,
        )(integrals, pair_blocks, occupied, metric)

    return whole
```

```python
import functools

import jax
import jax.numpy as jnp
from jax import lax
from jax.experimental import pallas as pl
from jax.experimental.pallas import tpu as pltpu
from jax.sharding import PartitionSpec as P

BS = 64
OCT = 8
EIGHTHS = (2, 3, 2, 1)
QT = 512
VMEM_LIMIT = 60 * 1024 * 1024


def gathered_plan(integrals, pair_blocks, occupied, metric, nbf):
    aux_rows, slot_count = integrals.shape[:2]
    occ_count = occupied.shape[1]
    rows_local = nbf // lax.axis_size("row")
    row_blocks = rows_local // BS
    metric_wide = metric.astype(jnp.float32)

    def add_slot(carry, slot):
        row_block = pair_blocks[0, slot]
        col_block = pair_blocks[1, slot]
        local_row = jnp.maximum(row_block, 0) % row_blocks
        local_col = jnp.maximum(col_block, 0) % (occupied.shape[0] // BS)
        tile = lax.dynamic_index_in_dim(integrals, slot, 1, False).reshape(aux_rows, BS, BS)
        cpart = lax.dynamic_slice_in_dim(occupied, local_col * BS, BS, 0)
        piece = jnp.einsum("pmn,ni->ipm", tile, cpart, preferred_element_type=jnp.float32)
        piece = jnp.where(row_block >= 0, piece, 0.0)
        current = lax.dynamic_slice_in_dim(carry, local_row * BS, BS, 2)
        return lax.dynamic_update_slice_in_dim(carry, current + piece, local_row * BS, 2), None

    start = jnp.zeros((occ_count, aux_rows, rows_local), jnp.float32)
    partials, _ = lax.scan(add_slot, start, jnp.arange(slot_count, dtype=jnp.int32))
    summed = lax.psum_scatter(partials, "col", scatter_dimension=1, tiled=True)
    half = lax.all_to_all(summed, ("aux", "col"), split_axis=0, concat_axis=1, tiled=True)
    highest = dict(precision=lax.Precision.HIGHEST, preferred_element_type=jnp.float32)
    fitted = jnp.einsum("qp,ipm->iqm", metric_wide, half, **highest)
    contrib = jnp.einsum("iqm,iqn->mn", fitted, lax.all_gather(fitted, "row", axis=2, tiled=True), **highest)
    return lax.psum_scatter(contrib, ("aux", "col"), scatter_dimension=1, tiled=True)


def contract_kernel(info_ref, occ_ref, x_ref, other_ref, mine_ref, xt_ref, w_ref):
    slots = x_ref.shape[1]
    half, _, octet, aux_rows = mine_ref.shape
    occ = 2 * half
    tall, wide = occ * octet, octet * BS
    f32 = dict(preferred_element_type=jnp.float32)

    @pl.when(pl.program_id(0) == 0)
    def _():
        spread = lax.broadcasted_iota(jnp.int32, (tall, occ), 0) // octet == lax.broadcasted_iota(
            jnp.int32, (tall, occ), 1
        )
        spread = spread.astype(jnp.bfloat16)
        tile = lax.broadcasted_iota(jnp.int32, (BS, wide), 1) % BS == lax.broadcasted_iota(jnp.int32, (BS, wide), 0)
        tile = tile.astype(jnp.bfloat16)
        keep = (
            lax.broadcasted_iota(jnp.int32, (tall, wide), 0) % octet
            == lax.broadcasted_iota(jnp.int32, (tall, wide), 1) // BS
        )

        def build(s, _):
            live = info_ref[1 + 2 * slots + s] > 0
            start = pl.multiple_of(info_ref[1 + slots + s] * BS, BS)
            coeffs = occ_ref[pl.ds(start, BS), :]
            rows = lax.dot_general(spread, coeffs, (((1,), (1,)), ((), ())), **f32).astype(jnp.bfloat16)
            full = jnp.dot(rows, tile, **f32)
            w_ref[s] = jnp.where(jnp.logical_and(keep, live), full, 0.0).astype(jnp.bfloat16)
            return 0

        lax.fori_loop(0, slots, build, 0)

    def turn(q, _):
        at = pl.ds(pl.multiple_of(q * 128, 128), 128)
        xt_ref[:, at] = pltpu.einshape("psk->spk", x_ref[at].astype(jnp.float32)).astype(jnp.bfloat16)
        return 0

    lax.fori_loop(0, aux_rows // 128, turn, 0)
    col = info_ref[0]
    for h, out_ref in ((1 - col, other_ref), (col, mine_ref)):
        out_ref[...] = jnp.zeros_like(out_ref)

        def one(s, _):
            w = w_ref[s, pl.ds(pl.multiple_of(h * half * octet, 16), half * octet)]
            piece = lax.dot_general(w, xt_ref[s], (((1,), (1,)), ((), ())), **f32)
            b = info_ref[1 + s]
            out_ref[:, b] = out_ref[:, b] + piece.reshape(half, octet, aux_rows)
            return 0

        lax.fori_loop(0, slots, one, 0)


def contract(info, occupied, integrals, lo, m, row_blocks):
    aux_rows, slots, _ = integrals.shape
    rows_in, occ = occupied.shape
    out = jax.ShapeDtypeStruct((occ // 2, row_blocks, m, aux_rows), jnp.float32)
    spec = pl.BlockSpec((occ // 2, row_blocks, OCT, aux_rows), lambda j, info: (0, 0, j, 0))
    return pl.pallas_call(
        contract_kernel,
        grid_spec=pltpu.PrefetchScalarGridSpec(
            num_scalar_prefetch=1,
            grid=(m // OCT,),
            in_specs=[
                pl.BlockSpec((rows_in, occ), lambda j, info: (0, 0)),
                pl.BlockSpec((aux_rows, slots, OCT * BS), lambda j, info: (0, 0, j + lo // OCT)),
            ],
            out_specs=[spec, spec],
            scratch_shapes=[
                pltpu.VMEM((slots, aux_rows, OCT * BS), jnp.bfloat16),
                pltpu.VMEM((slots, occ * OCT, OCT * BS), jnp.bfloat16),
            ],
        ),
        out_shape=[out, out],
        compiler_params=pltpu.CompilerParams(vmem_limit_bytes=VMEM_LIMIT),
        cost_estimate=pl.CostEstimate(
            flops=2 * slots * aux_rows * occ * OCT * m * BS,
            bytes_accessed=2 * slots * aux_rows * m * BS + 4 * occ * row_blocks * m * aux_rows,
            transcendentals=0,
        ),
        name="contract",
    )(info, occupied, integrals)


def combine_kernel(me_ref, mine_ref, got_ref, *out_refs):
    me = me_ref[0]
    for d, out_ref in enumerate(out_refs):
        dest = lax.bitwise_xor(me, d)
        out_ref[...] = mine_ref[dest] + got_ref[dest]


def combine(me, mine, got):
    group, share, rows, aux_rows = mine.shape
    piece = jax.ShapeDtypeStruct((share, rows, aux_rows), jnp.float32)
    vmem = pl.BlockSpec(memory_space=pltpu.VMEM)
    return pl.pallas_call(
        combine_kernel,
        in_specs=[pl.BlockSpec(memory_space=pltpu.SMEM), vmem, vmem],
        out_specs=[vmem] * group,
        out_shape=[piece] * group,
        compiler_params=pltpu.CompilerParams(vmem_limit_bytes=VMEM_LIMIT),
        cost_estimate=pl.CostEstimate(flops=mine.size, bytes_accessed=12 * mine.size, transcendentals=0),
        name="combine",
    )(me, mine, got)


def high_low(x):
    high = x.astype(jnp.bfloat16)
    return high, (x - high.astype(jnp.float32)).astype(jnp.bfloat16)


def consume_kernel(me_ref, *refs, n_row, starts, sizes, last):
    c = len(sizes) - 1
    refs = list(refs)
    n_pieces = len(refs) - 4 - 2 * c - (1 if c else 0) - (0 if last else 2)
    pieces, refs = refs[:n_pieces], refs[n_pieces:]
    m_ref, refs = refs[0], refs[1:]
    earlier, refs = refs[: 2 * c], refs[2 * c :]
    if c:
        k_in, refs = refs[0], refs[1:]
    if not last:
        fh_ref, fl_ref, refs = refs[0], refs[1], refs[2:]
    k_ref, h_ref, cross_ref = refs
    me = me_ref[0]
    share, rows, aux_rows = pieces[0].shape
    total = rows * n_row
    blocks = k_ref.shape[0]
    j = pl.program_id(0)

    @pl.when(j == 0)
    def _():
        if c:
            k_ref[...] = k_in[...]
        else:
            k_ref[...] = jnp.zeros_like(k_ref)
        cross_ref[...] = jnp.zeros_like(cross_ref)
        for d, piece in enumerate(pieces):
            source = lax.bitwise_xor(me, d)
            aux = lax.div(source, n_row)
            row = lax.rem(source, n_row)
            lanes = pl.ds(pl.multiple_of(aux * aux_rows, 128), aux_rows)
            for t in range(share):
                high, low = high_low(piece[t])
                at = pl.multiple_of(row * rows, 16)
                h_ref[pl.ds(at + t * total, rows), lanes] = high
                h_ref[pl.ds(at + (share + t) * total, rows), lanes] = low

    f32 = dict(preferred_element_type=jnp.float32)
    both = jnp.dot(h_ref[...], m_ref[...], **f32)
    fh, fl = high_low(both[: share * total] + both[share * total :])
    if not last:
        fh_ref[...] = fh.reshape(fh_ref.shape)
        fl_ref[...] = fl.reshape(fl_ref.shape)

    def outer(a, b):
        a, b = jnp.concatenate(a, 1), jnp.concatenate(b, 1)
        return lax.dot_general(a, b, (((1,), (1,)), ((), ())), **f32)

    def part(ci, cj):
        rows_at = pl.ds(starts[ci], sizes[ci])
        lanes_at = pl.ds(blocks * starts[cj], blocks * sizes[cj])
        return (slice(None), rows_at, lanes_at), (blocks, sizes[ci], blocks * sizes[cj])

    ah = [fh[t * total : (t + 1) * total] for t in range(share)]
    al = [fl[t * total : (t + 1) * total] for t in range(share)]
    at, shape = part(c, c)
    k_ref[at] = k_ref[at] + outer(ah, ah).reshape(shape)
    cross_ref[...] = cross_ref[...] + outer(ah, al)
    for e in range(c):
        bh = [earlier[2 * e][t] for t in range(share)]
        bl = [earlier[2 * e + 1][t] for t in range(share)]
        at, shape = part(c, e)
        k_ref[at] = k_ref[at] + outer(ah + ah + al, bh + bl + bh).reshape(shape)

    @pl.when(j == pl.num_programs(0) - 1)
    def _():
        at, shape = part(c, c)
        cross = cross_ref[...]
        k_ref[at] = k_ref[at] + (cross + cross.T).reshape(shape)
        for e in range(c):
            at, _ = part(c, e)
            turned = k_ref[at].reshape(total, -1).T
            at, shape = part(e, c)
            k_ref[at] = turned.reshape(shape)


def consume(me, pieces, metric, earlier, k_so_far, n_row, nbf, starts, sizes, last):
    share, rows, aux_rows = pieces[0].shape
    total = rows * n_row
    n_aux_all = metric.shape[0]
    once = pl.Buffered(1)
    whole = pl.BlockSpec((share, rows, aux_rows), lambda j: (0, 0, 0), pipeline_mode=once)
    in_specs = [pl.BlockSpec(memory_space=pltpu.SMEM)] + [whole] * len(pieces)
    in_specs.append(pl.BlockSpec((n_aux_all, QT), lambda j: (0, j)))
    in_specs += [pl.BlockSpec((f.shape[0], f.shape[1], QT), lambda j: (0, 0, j)) for f in earlier]
    k_shape = (nbf // BS, BS, nbf)
    k_spec = pl.BlockSpec(k_shape, lambda j: (0, 0, 0), pipeline_mode=once)
    args = [me, *pieces, metric, *earlier]
    if k_so_far is not None:
        in_specs.append(k_spec)
        args.append(k_so_far)
    out_specs, out_shape = [], []
    if not last:
        out_specs += [pl.BlockSpec((share, total, QT), lambda j: (0, 0, j))] * 2
        out_shape += [jax.ShapeDtypeStruct((share, total, n_aux_all), jnp.bfloat16)] * 2
    out_specs.append(k_spec)
    out_shape.append(jax.ShapeDtypeStruct(k_shape, jnp.float32))
    scratch = [pltpu.VMEM((2 * share * total, n_aux_all), jnp.bfloat16), pltpu.VMEM((total, total), jnp.float32)]
    done = nbf // BS * sum(sizes)
    return pl.pallas_call(
        functools.partial(consume_kernel, n_row=n_row, starts=starts, sizes=sizes, last=last),
        grid=(n_aux_all // QT,),
        in_specs=in_specs,
        out_specs=out_specs,
        out_shape=out_shape,
        scratch_shapes=scratch,
        compiler_params=pltpu.CompilerParams(vmem_limit_bytes=VMEM_LIMIT),
        cost_estimate=pl.CostEstimate(
            flops=4 * share * total * n_aux_all * n_aux_all + 6 * share * total * done * n_aux_all,
            bytes_accessed=2 * metric.size + 4 * share * total * n_aux_all,
            transcendentals=0,
        ),
        name="consume",
    )(*args)


def swap_sum(parts, axis, n):
    me = lax.axis_index(axis)
    own = lax.dynamic_index_in_dim(parts, me, 0, False)
    for d in range(n - 1, 0, -1):
        given = lax.dynamic_index_in_dim(parts, me ^ d, 0, False)
        own = own + lax.ppermute(given, axis, [(s, s ^ d) for s in range(n)])
    return own


def body(integrals, pair_blocks, occupied, metric, nbf):
    n_aux, n_row, n_col = lax.axis_size("aux"), lax.axis_size("row"), lax.axis_size("col")
    occ = occupied.shape[1]
    devices = n_aux * n_row * n_col
    group = n_aux * n_row
    aux_rows, _, _ = integrals.shape
    groups = n_aux * n_col
    fits = (
        n_col == 2
        and occ % devices == 0
        and aux_rows % 128 == 0
        and group & (group - 1) == 0
        and nbf % (groups * BS) == 0
        and nbf // BS * OCT % 128 == 0
        and metric.shape[0] % QT == 0
    )
    if not fits:
        return gathered_plan(integrals, pair_blocks, occupied, metric, nbf)
    row_blocks = nbf // n_row // BS
    share = occ // devices
    me = lax.axis_index("aux") * n_row + lax.axis_index("row")
    me_array = me.reshape(1).astype(jnp.int32)

    live = (pair_blocks[0] >= 0).astype(jnp.int32)
    rows = jnp.maximum(pair_blocks[0], 0) % row_blocks
    cols = jnp.maximum(pair_blocks[1], 0) % (occupied.shape[0] // BS)
    info = jnp.concatenate([lax.axis_index("col").reshape(1).astype(jnp.int32), rows, cols, live]).astype(jnp.int32)

    sizes = tuple(e * BS // 8 for e in EIGHTHS)
    starts = tuple(sum(sizes[:c]) for c in range(len(sizes)))
    count = len(sizes)
    arrived, earlier, total = [], [], None

    def use(c, me_array):
        last = c == count - 1
        return consume(me_array, arrived[c], metric, earlier, total, n_row, nbf, starts[: c + 1], sizes[: c + 1], last)

    for c in range(count):
        if c == count - 1:
            *fitted, total = use(0, me_array)
            earlier += fitted
            info, total = lax.optimization_barrier((info, total))
        other, mine = contract(info, occupied, integrals, starts[c], sizes[c], row_blocks)
        got = lax.ppermute(other, "col", [(0, 1), (1, 0)])
        shape = (group, share, row_blocks * sizes[c], aux_rows)
        pieces = list(combine(me_array, mine.reshape(shape), got.reshape(shape)))
        info, me_array, pieces[0] = lax.optimization_barrier((info, me_array, pieces[0]))
        sent = [None] * group
        for d in sorted(range(group), key=lambda d: -bin(d).count("1")):
            pairs = [(s, s ^ d) for s in range(group)]
            sent[d] = pieces[d] if d == 0 else lax.ppermute(pieces[d], ("aux", "row"), pairs)
        arrived.append(sent)

    for c in range(1, count):
        *fitted, total = use(c, me_array)
        earlier += fitted

    halves = total.reshape(n_aux, n_col, -1, nbf)
    col = lax.axis_index("col")
    given = lax.dynamic_index_in_dim(halves, 1 - col, 1, False)
    part = lax.dynamic_index_in_dim(halves, col, 1, False) + lax.ppermute(given, "col", [(0, 1), (1, 0)])
    part = swap_sum(part, "aux", n_aux)
    blocks = nbf // BS
    part = part.T
    strips = [part[blocks * lo : blocks * (lo + m)].reshape(blocks, m, -1) for lo, m in zip(starts, sizes)]
    part = jnp.concatenate(strips, 1).reshape(n_row, nbf // n_row, -1)
    return swap_sum(part, "row", n_row)


def solution(mesh):
    def local(*args, nbf):
        return body(*args, nbf)

    def whole(integrals, pair_blocks, occupied, metric):
        nbf = occupied.shape[0]
        return jax.shard_map(
            functools.partial(local, nbf=nbf),
            mesh=mesh,
            in_specs=(P("aux", ("row", "col"), None), P(None, ("row", "col")), P("col", None), P()),
            out_specs=P("row", ("aux", "col")),
            check_vma=False,
        )(integrals, pair_blocks, occupied, metric)

    return whole
```

```python
import functools

import jax
import jax.numpy as jnp
from jax import lax
from jax.experimental import pallas as pl
from jax.experimental.pallas import tpu as pltpu
from jax.sharding import PartitionSpec as P

BS = 64
OCT = 8
EIGHTHS = (2, 2, 3, 1)
QT = 512
VMEM_LIMIT = 60 * 1024 * 1024


def gathered_plan(integrals, pair_blocks, occupied, metric, nbf):
    aux_rows, slot_count = integrals.shape[:2]
    occ_count = occupied.shape[1]
    rows_local = nbf // lax.axis_size("row")
    row_blocks = rows_local // BS
    metric_wide = metric.astype(jnp.float32)

    def add_slot(carry, slot):
        row_block = pair_blocks[0, slot]
        col_block = pair_blocks[1, slot]
        local_row = jnp.maximum(row_block, 0) % row_blocks
        local_col = jnp.maximum(col_block, 0) % (occupied.shape[0] // BS)
        tile = lax.dynamic_index_in_dim(integrals, slot, 1, False).reshape(aux_rows, BS, BS)
        cpart = lax.dynamic_slice_in_dim(occupied, local_col * BS, BS, 0)
        piece = jnp.einsum("pmn,ni->ipm", tile, cpart, preferred_element_type=jnp.float32)
        piece = jnp.where(row_block >= 0, piece, 0.0)
        current = lax.dynamic_slice_in_dim(carry, local_row * BS, BS, 2)
        return lax.dynamic_update_slice_in_dim(carry, current + piece, local_row * BS, 2), None

    start = jnp.zeros((occ_count, aux_rows, rows_local), jnp.float32)
    partials, _ = lax.scan(add_slot, start, jnp.arange(slot_count, dtype=jnp.int32))
    summed = lax.psum_scatter(partials, "col", scatter_dimension=1, tiled=True)
    half = lax.all_to_all(summed, ("aux", "col"), split_axis=0, concat_axis=1, tiled=True)
    highest = dict(precision=lax.Precision.HIGHEST, preferred_element_type=jnp.float32)
    fitted = jnp.einsum("qp,ipm->iqm", metric_wide, half, **highest)
    contrib = jnp.einsum("iqm,iqn->mn", fitted, lax.all_gather(fitted, "row", axis=2, tiled=True), **highest)
    return lax.psum_scatter(contrib, ("aux", "col"), scatter_dimension=1, tiled=True)


def contract_kernel(info_ref, occ_ref, x_ref, other_ref, mine_ref, xt_ref, w_ref):
    slots = x_ref.shape[1]
    half, _, octet, aux_rows = mine_ref.shape
    occ = 2 * half
    tall, wide = occ * octet, octet * BS
    f32 = dict(preferred_element_type=jnp.float32)

    @pl.when(pl.program_id(0) == 0)
    def _():
        spread = lax.broadcasted_iota(jnp.int32, (tall, occ), 0) // octet == lax.broadcasted_iota(
            jnp.int32, (tall, occ), 1
        )
        spread = spread.astype(jnp.bfloat16)
        tile = lax.broadcasted_iota(jnp.int32, (BS, wide), 1) % BS == lax.broadcasted_iota(jnp.int32, (BS, wide), 0)
        tile = tile.astype(jnp.bfloat16)
        keep = (
            lax.broadcasted_iota(jnp.int32, (tall, wide), 0) % octet
            == lax.broadcasted_iota(jnp.int32, (tall, wide), 1) // BS
        )

        def build(s, _):
            live = info_ref[1 + 2 * slots + s] > 0
            start = pl.multiple_of(info_ref[1 + slots + s] * BS, BS)
            coeffs = occ_ref[pl.ds(start, BS), :]
            rows = lax.dot_general(spread, coeffs, (((1,), (1,)), ((), ())), **f32).astype(jnp.bfloat16)
            full = jnp.dot(rows, tile, **f32)
            w_ref[s] = jnp.where(jnp.logical_and(keep, live), full, 0.0).astype(jnp.bfloat16)
            return 0

        lax.fori_loop(0, slots, build, 0)

    def turn(q, _):
        at = pl.ds(pl.multiple_of(q * 128, 128), 128)
        xt_ref[:, at] = pltpu.einshape("psk->spk", x_ref[at].astype(jnp.float32)).astype(jnp.bfloat16)
        return 0

    lax.fori_loop(0, aux_rows // 128, turn, 0)
    col = info_ref[0]
    for h, out_ref in ((1 - col, other_ref), (col, mine_ref)):
        out_ref[...] = jnp.zeros_like(out_ref)

        def one(s, _):
            w = w_ref[s, pl.ds(pl.multiple_of(h * half * octet, 16), half * octet)]
            piece = lax.dot_general(w, xt_ref[s], (((1,), (1,)), ((), ())), **f32)
            b = info_ref[1 + s]
            out_ref[:, b] = out_ref[:, b] + piece.reshape(half, octet, aux_rows)
            return 0

        lax.fori_loop(0, slots, one, 0)


def contract(info, occupied, integrals, lo, m, row_blocks):
    aux_rows, slots, _ = integrals.shape
    rows_in, occ = occupied.shape
    out = jax.ShapeDtypeStruct((occ // 2, row_blocks, m, aux_rows), jnp.float32)
    spec = pl.BlockSpec((occ // 2, row_blocks, OCT, aux_rows), lambda j, info: (0, 0, j, 0))
    return pl.pallas_call(
        contract_kernel,
        grid_spec=pltpu.PrefetchScalarGridSpec(
            num_scalar_prefetch=1,
            grid=(m // OCT,),
            in_specs=[
                pl.BlockSpec((rows_in, occ), lambda j, info: (0, 0)),
                pl.BlockSpec((aux_rows, slots, OCT * BS), lambda j, info: (0, 0, j + lo // OCT)),
            ],
            out_specs=[spec, spec],
            scratch_shapes=[
                pltpu.VMEM((slots, aux_rows, OCT * BS), jnp.bfloat16),
                pltpu.VMEM((slots, occ * OCT, OCT * BS), jnp.bfloat16),
            ],
        ),
        out_shape=[out, out],
        compiler_params=pltpu.CompilerParams(vmem_limit_bytes=VMEM_LIMIT),
        cost_estimate=pl.CostEstimate(
            flops=2 * slots * aux_rows * occ * OCT * m * BS,
            bytes_accessed=2 * slots * aux_rows * m * BS + 4 * occ * row_blocks * m * aux_rows,
            transcendentals=0,
        ),
        name="contract",
    )(info, occupied, integrals)


def combine_kernel(me_ref, mine_ref, got_ref, *out_refs):
    me = me_ref[0]
    for d, out_ref in enumerate(out_refs):
        dest = lax.bitwise_xor(me, d)
        out_ref[...] = mine_ref[dest] + got_ref[dest]


def combine(me, mine, got):
    group, share, rows, aux_rows = mine.shape
    piece = jax.ShapeDtypeStruct((share, rows, aux_rows), jnp.float32)
    vmem = pl.BlockSpec(memory_space=pltpu.VMEM)
    return pl.pallas_call(
        combine_kernel,
        in_specs=[pl.BlockSpec(memory_space=pltpu.SMEM), vmem, vmem],
        out_specs=[vmem] * group,
        out_shape=[piece] * group,
        compiler_params=pltpu.CompilerParams(vmem_limit_bytes=VMEM_LIMIT),
        cost_estimate=pl.CostEstimate(flops=mine.size, bytes_accessed=12 * mine.size, transcendentals=0),
        name="combine",
    )(me, mine, got)


def high_low(x):
    high = x.astype(jnp.bfloat16)
    return high, (x - high.astype(jnp.float32)).astype(jnp.bfloat16)


def consume_kernel(me_ref, *refs, n_row, starts, sizes, last):
    c = len(sizes) - 1
    refs = list(refs)
    n_pieces = len(refs) - 4 - 2 * c - (1 if c else 0) - (0 if last else 2)
    pieces, refs = refs[:n_pieces], refs[n_pieces:]
    m_ref, refs = refs[0], refs[1:]
    earlier, refs = refs[: 2 * c], refs[2 * c :]
    if c:
        k_in, refs = refs[0], refs[1:]
    if not last:
        fh_ref, fl_ref, refs = refs[0], refs[1], refs[2:]
    k_ref, h_ref, cross_ref = refs
    me = me_ref[0]
    share, rows, aux_rows = pieces[0].shape
    total = rows * n_row
    blocks = k_ref.shape[0]
    j = pl.program_id(0)

    @pl.when(j == 0)
    def _():
        if c:
            k_ref[...] = k_in[...]
        else:
            k_ref[...] = jnp.zeros_like(k_ref)
        cross_ref[...] = jnp.zeros_like(cross_ref)
        for d, piece in enumerate(pieces):
            source = lax.bitwise_xor(me, d)
            aux = lax.div(source, n_row)
            row = lax.rem(source, n_row)
            lanes = pl.ds(pl.multiple_of(aux * aux_rows, 128), aux_rows)
            for t in range(share):
                high, low = high_low(piece[t])
                at = pl.multiple_of(row * rows, 16)
                h_ref[pl.ds(at + t * total, rows), lanes] = high
                h_ref[pl.ds(at + (share + t) * total, rows), lanes] = low

    f32 = dict(preferred_element_type=jnp.float32)
    both = jnp.dot(h_ref[...], m_ref[...], **f32)
    fh, fl = high_low(both[: share * total] + both[share * total :])
    if not last:
        fh_ref[...] = fh.reshape(fh_ref.shape)
        fl_ref[...] = fl.reshape(fl_ref.shape)

    def outer(a, b):
        a, b = jnp.concatenate(a, 1), jnp.concatenate(b, 1)
        return lax.dot_general(a, b, (((1,), (1,)), ((), ())), **f32)

    def part(ci, cj):
        rows_at = pl.ds(starts[ci], sizes[ci])
        lanes_at = pl.ds(blocks * starts[cj], blocks * sizes[cj])
        return (slice(None), rows_at, lanes_at), (blocks, sizes[ci], blocks * sizes[cj])

    ah = [fh[t * total : (t + 1) * total] for t in range(share)]
    al = [fl[t * total : (t + 1) * total] for t in range(share)]
    at, shape = part(c, c)
    k_ref[at] = k_ref[at] + outer(ah, ah).reshape(shape)
    cross_ref[...] = cross_ref[...] + outer(ah, al)
    for e in range(c):
        bh = [earlier[2 * e][t] for t in range(share)]
        bl = [earlier[2 * e + 1][t] for t in range(share)]
        at, shape = part(c, e)
        k_ref[at] = k_ref[at] + outer(ah + ah + al, bh + bl + bh).reshape(shape)

    @pl.when(j == pl.num_programs(0) - 1)
    def _():
        at, shape = part(c, c)
        cross = cross_ref[...]
        k_ref[at] = k_ref[at] + (cross + cross.T).reshape(shape)
        for e in range(c):
            at, _ = part(c, e)
            turned = k_ref[at].reshape(total, -1).T
            at, shape = part(e, c)
            k_ref[at] = turned.reshape(shape)


def consume(me, pieces, metric, earlier, k_so_far, n_row, nbf, starts, sizes, last):
    share, rows, aux_rows = pieces[0].shape
    total = rows * n_row
    n_aux_all = metric.shape[0]
    once = pl.Buffered(1)
    whole = pl.BlockSpec((share, rows, aux_rows), lambda j: (0, 0, 0), pipeline_mode=once)
    in_specs = [pl.BlockSpec(memory_space=pltpu.SMEM)] + [whole] * len(pieces)
    in_specs.append(pl.BlockSpec((n_aux_all, QT), lambda j: (0, j)))
    in_specs += [pl.BlockSpec((f.shape[0], f.shape[1], QT), lambda j: (0, 0, j)) for f in earlier]
    k_shape = (nbf // BS, BS, nbf)
    k_spec = pl.BlockSpec(k_shape, lambda j: (0, 0, 0), pipeline_mode=once)
    args = [me, *pieces, metric, *earlier]
    if k_so_far is not None:
        in_specs.append(k_spec)
        args.append(k_so_far)
    out_specs, out_shape = [], []
    if not last:
        out_specs += [pl.BlockSpec((share, total, QT), lambda j: (0, 0, j))] * 2
        out_shape += [jax.ShapeDtypeStruct((share, total, n_aux_all), jnp.bfloat16)] * 2
    out_specs.append(k_spec)
    out_shape.append(jax.ShapeDtypeStruct(k_shape, jnp.float32))
    scratch = [pltpu.VMEM((2 * share * total, n_aux_all), jnp.bfloat16), pltpu.VMEM((total, total), jnp.float32)]
    done = nbf // BS * sum(sizes)
    return pl.pallas_call(
        functools.partial(consume_kernel, n_row=n_row, starts=starts, sizes=sizes, last=last),
        grid=(n_aux_all // QT,),
        in_specs=in_specs,
        out_specs=out_specs,
        out_shape=out_shape,
        scratch_shapes=scratch,
        compiler_params=pltpu.CompilerParams(vmem_limit_bytes=VMEM_LIMIT),
        cost_estimate=pl.CostEstimate(
            flops=4 * share * total * n_aux_all * n_aux_all + 6 * share * total * done * n_aux_all,
            bytes_accessed=2 * metric.size + 4 * share * total * n_aux_all,
            transcendentals=0,
        ),
        name="consume",
    )(*args)


def swap_sum(parts, axis, n):
    me = lax.axis_index(axis)
    own = lax.dynamic_index_in_dim(parts, me, 0, False)
    for d in range(n - 1, 0, -1):
        given = lax.dynamic_index_in_dim(parts, me ^ d, 0, False)
        own = own + lax.ppermute(given, axis, [(s, s ^ d) for s in range(n)])
    return own


def body(integrals, pair_blocks, occupied, metric, nbf):
    n_aux, n_row, n_col = lax.axis_size("aux"), lax.axis_size("row"), lax.axis_size("col")
    occ = occupied.shape[1]
    devices = n_aux * n_row * n_col
    group = n_aux * n_row
    aux_rows, _, _ = integrals.shape
    groups = n_aux * n_col
    fits = (
        n_col == 2
        and occ % devices == 0
        and aux_rows % 128 == 0
        and group & (group - 1) == 0
        and nbf % (groups * BS) == 0
        and nbf // BS * OCT % 128 == 0
        and metric.shape[0] % QT == 0
    )
    if not fits:
        return gathered_plan(integrals, pair_blocks, occupied, metric, nbf)
    row_blocks = nbf // n_row // BS
    share = occ // devices
    me = lax.axis_index("aux") * n_row + lax.axis_index("row")
    me_array = me.reshape(1).astype(jnp.int32)

    live = (pair_blocks[0] >= 0).astype(jnp.int32)
    rows = jnp.maximum(pair_blocks[0], 0) % row_blocks
    cols = jnp.maximum(pair_blocks[1], 0) % (occupied.shape[0] // BS)
    info = jnp.concatenate([lax.axis_index("col").reshape(1).astype(jnp.int32), rows, cols, live]).astype(jnp.int32)

    sizes = tuple(e * BS // 8 for e in EIGHTHS)
    starts = tuple(sum(sizes[:c]) for c in range(len(sizes)))
    count = len(sizes)
    arrived, earlier, total = [], [], None

    def use(c, me_array):
        last = c == count - 1
        return consume(me_array, arrived[c], metric, earlier, total, n_row, nbf, starts[: c + 1], sizes[: c + 1], last)

    for c in range(count):
        if c == count - 1:
            for early in range(count - 2):
                *fitted, total = use(early, me_array)
                earlier += fitted
            info, total = lax.optimization_barrier((info, total))
        other, mine = contract(info, occupied, integrals, starts[c], sizes[c], row_blocks)
        got = lax.ppermute(other, "col", [(0, 1), (1, 0)])
        shape = (group, share, row_blocks * sizes[c], aux_rows)
        pieces = list(combine(me_array, mine.reshape(shape), got.reshape(shape)))
        info, me_array, pieces[0] = lax.optimization_barrier((info, me_array, pieces[0]))
        sent = [None] * group
        for d in sorted(range(group), key=lambda d: -bin(d).count("1")):
            pairs = [(s, s ^ d) for s in range(group)]
            sent[d] = pieces[d] if d == 0 else lax.ppermute(pieces[d], ("aux", "row"), pairs)
        arrived.append(sent)

    for c in range(count - 2, count):
        *fitted, total = use(c, me_array)
        earlier += fitted

    halves = total.reshape(n_aux, n_col, -1, nbf)
    col = lax.axis_index("col")
    given = lax.dynamic_index_in_dim(halves, 1 - col, 1, False)
    part = lax.dynamic_index_in_dim(halves, col, 1, False) + lax.ppermute(given, "col", [(0, 1), (1, 0)])
    part = swap_sum(part, "aux", n_aux)
    blocks = nbf // BS
    part = part.T
    strips = [part[blocks * lo : blocks * (lo + m)].reshape(blocks, m, -1) for lo, m in zip(starts, sizes)]
    part = jnp.concatenate(strips, 1).reshape(n_row, nbf // n_row, -1)
    return swap_sum(part, "row", n_row)


def solution(mesh):
    def local(*args, nbf):
        return body(*args, nbf)

    def whole(integrals, pair_blocks, occupied, metric):
        nbf = occupied.shape[0]
        return jax.shard_map(
            functools.partial(local, nbf=nbf),
            mesh=mesh,
            in_specs=(P("aux", ("row", "col"), None), P(None, ("row", "col")), P("col", None), P()),
            out_specs=P("row", ("aux", "col")),
            check_vma=False,
        )(integrals, pair_blocks, occupied, metric)

    return whole
```

```python
import functools

import jax
import jax.numpy as jnp
from jax import lax
from jax.experimental import pallas as pl
from jax.experimental.pallas import tpu as pltpu
from jax.sharding import PartitionSpec as P

BS = 64
OCT = 8
EIGHTHS = (2, 3, 2, 1)
QT = 512
VMEM_LIMIT = 60 * 1024 * 1024


def gathered_plan(integrals, pair_blocks, occupied, metric, nbf):
    aux_rows, slot_count = integrals.shape[:2]
    occ_count = occupied.shape[1]
    rows_local = nbf // lax.axis_size("row")
    row_blocks = rows_local // BS
    metric_wide = metric.astype(jnp.float32)

    def add_slot(carry, slot):
        row_block = pair_blocks[0, slot]
        col_block = pair_blocks[1, slot]
        local_row = jnp.maximum(row_block, 0) % row_blocks
        local_col = jnp.maximum(col_block, 0) % (occupied.shape[0] // BS)
        tile = lax.dynamic_index_in_dim(integrals, slot, 1, False).reshape(aux_rows, BS, BS)
        cpart = lax.dynamic_slice_in_dim(occupied, local_col * BS, BS, 0)
        piece = jnp.einsum("pmn,ni->ipm", tile, cpart, preferred_element_type=jnp.float32)
        piece = jnp.where(row_block >= 0, piece, 0.0)
        current = lax.dynamic_slice_in_dim(carry, local_row * BS, BS, 2)
        return lax.dynamic_update_slice_in_dim(carry, current + piece, local_row * BS, 2), None

    start = jnp.zeros((occ_count, aux_rows, rows_local), jnp.float32)
    partials, _ = lax.scan(add_slot, start, jnp.arange(slot_count, dtype=jnp.int32))
    summed = lax.psum_scatter(partials, "col", scatter_dimension=1, tiled=True)
    half = lax.all_to_all(summed, ("aux", "col"), split_axis=0, concat_axis=1, tiled=True)
    highest = dict(precision=lax.Precision.HIGHEST, preferred_element_type=jnp.float32)
    fitted = jnp.einsum("qp,ipm->iqm", metric_wide, half, **highest)
    contrib = jnp.einsum("iqm,iqn->mn", fitted, lax.all_gather(fitted, "row", axis=2, tiled=True), **highest)
    return lax.psum_scatter(contrib, ("aux", "col"), scatter_dimension=1, tiled=True)


def contract_kernel(info_ref, occ_ref, x_ref, other_ref, mine_ref, xt_ref, w_ref):
    slots = x_ref.shape[1]
    half, _, octet, aux_rows = mine_ref.shape
    occ = 2 * half
    tall, wide = occ * octet, octet * BS
    f32 = dict(preferred_element_type=jnp.float32)

    @pl.when(pl.program_id(0) == 0)
    def _():
        first = (1 - info_ref[0]) * half
        orbital = (lax.broadcasted_iota(jnp.int32, (tall, occ), 0) // octet + first) % occ
        spread = orbital == lax.broadcasted_iota(jnp.int32, (tall, occ), 1)
        spread = spread.astype(jnp.bfloat16)
        tile = lax.broadcasted_iota(jnp.int32, (BS, wide), 1) % BS == lax.broadcasted_iota(jnp.int32, (BS, wide), 0)
        tile = tile.astype(jnp.bfloat16)
        keep = (
            lax.broadcasted_iota(jnp.int32, (tall, wide), 0) % octet
            == lax.broadcasted_iota(jnp.int32, (tall, wide), 1) // BS
        )

        def build(s, _):
            live = info_ref[1 + 2 * slots + s] > 0
            start = pl.multiple_of(info_ref[1 + slots + s] * BS, BS)
            coeffs = occ_ref[pl.ds(start, BS), :]
            rows = lax.dot_general(spread, coeffs, (((1,), (1,)), ((), ())), **f32).astype(jnp.bfloat16)
            full = jnp.dot(rows, tile, **f32)
            w_ref[s] = jnp.where(jnp.logical_and(keep, live), full, 0.0).astype(jnp.bfloat16)
            return 0

        lax.fori_loop(0, slots, build, 0)

    def turn(q, _):
        at = pl.ds(pl.multiple_of(q * 128, 128), 128)
        xt_ref[:, at] = pltpu.einshape("psk->spk", x_ref[at].astype(jnp.float32)).astype(jnp.bfloat16)
        return 0

    lax.fori_loop(0, aux_rows // 128, turn, 0)
    other_ref[...] = jnp.zeros_like(other_ref)
    mine_ref[...] = jnp.zeros_like(mine_ref)

    def one(s, _):
        piece = lax.dot_general(w_ref[s], xt_ref[s], (((1,), (1,)), ((), ())), **f32)
        b = info_ref[1 + s]
        other_ref[:, b] = other_ref[:, b] + piece[: half * octet].reshape(half, octet, aux_rows)
        mine_ref[:, b] = mine_ref[:, b] + piece[half * octet :].reshape(half, octet, aux_rows)
        return 0

    lax.fori_loop(0, slots, one, 0)


def contract(info, occupied, integrals, lo, m, row_blocks):
    aux_rows, slots, _ = integrals.shape
    rows_in, occ = occupied.shape
    out = jax.ShapeDtypeStruct((occ // 2, row_blocks, m, aux_rows), jnp.float32)
    spec = pl.BlockSpec((occ // 2, row_blocks, OCT, aux_rows), lambda j, info: (0, 0, j, 0))
    return pl.pallas_call(
        contract_kernel,
        grid_spec=pltpu.PrefetchScalarGridSpec(
            num_scalar_prefetch=1,
            grid=(m // OCT,),
            in_specs=[
                pl.BlockSpec((rows_in, occ), lambda j, info: (0, 0)),
                pl.BlockSpec((aux_rows, slots, OCT * BS), lambda j, info: (0, 0, j + lo // OCT)),
            ],
            out_specs=[spec, spec],
            scratch_shapes=[
                pltpu.VMEM((slots, aux_rows, OCT * BS), jnp.bfloat16),
                pltpu.VMEM((slots, occ * OCT, OCT * BS), jnp.bfloat16),
            ],
        ),
        out_shape=[out, out],
        compiler_params=pltpu.CompilerParams(vmem_limit_bytes=VMEM_LIMIT),
        cost_estimate=pl.CostEstimate(
            flops=2 * slots * aux_rows * occ * OCT * m * BS,
            bytes_accessed=2 * slots * aux_rows * m * BS + 4 * occ * row_blocks * m * aux_rows,
            transcendentals=0,
        ),
        name="contract",
    )(info, occupied, integrals)


def combine_kernel(me_ref, mine_ref, got_ref, *out_refs):
    me = me_ref[0]
    for d, out_ref in enumerate(out_refs):
        dest = lax.bitwise_xor(me, d)
        out_ref[...] = mine_ref[dest] + got_ref[dest]


def combine(me, mine, got):
    group, share, rows, aux_rows = mine.shape
    piece = jax.ShapeDtypeStruct((share, rows, aux_rows), jnp.float32)
    vmem = pl.BlockSpec(memory_space=pltpu.VMEM)
    return pl.pallas_call(
        combine_kernel,
        in_specs=[pl.BlockSpec(memory_space=pltpu.SMEM), vmem, vmem],
        out_specs=[vmem] * group,
        out_shape=[piece] * group,
        compiler_params=pltpu.CompilerParams(vmem_limit_bytes=VMEM_LIMIT),
        cost_estimate=pl.CostEstimate(flops=mine.size, bytes_accessed=12 * mine.size, transcendentals=0),
        name="combine",
    )(me, mine, got)


def high_low(x):
    high = x.astype(jnp.bfloat16)
    return high, (x - high.astype(jnp.float32)).astype(jnp.bfloat16)


def consume_kernel(me_ref, *refs, n_row, starts, sizes, last):
    c = len(sizes) - 1
    refs = list(refs)
    n_pieces = len(refs) - 4 - 2 * c - (1 if c else 0) - (0 if last else 2)
    pieces, refs = refs[:n_pieces], refs[n_pieces:]
    m_ref, refs = refs[0], refs[1:]
    earlier, refs = refs[: 2 * c], refs[2 * c :]
    if c:
        k_in, refs = refs[0], refs[1:]
    if not last:
        fh_ref, fl_ref, refs = refs[0], refs[1], refs[2:]
    k_ref, h_ref, cross_ref = refs
    me = me_ref[0]
    share, rows, aux_rows = pieces[0].shape
    total = rows * n_row
    blocks = k_ref.shape[0]
    j = pl.program_id(0)

    @pl.when(j == 0)
    def _():
        if c:
            k_ref[...] = k_in[...]
        else:
            k_ref[...] = jnp.zeros_like(k_ref)
        cross_ref[...] = jnp.zeros_like(cross_ref)
        for d, piece in enumerate(pieces):
            source = lax.bitwise_xor(me, d)
            aux = lax.div(source, n_row)
            row = lax.rem(source, n_row)
            lanes = pl.ds(pl.multiple_of(aux * aux_rows, 128), aux_rows)
            for t in range(share):
                high, low = high_low(piece[t])
                at = pl.multiple_of(row * rows, 16)
                h_ref[pl.ds(at + t * total, rows), lanes] = high
                h_ref[pl.ds(at + (share + t) * total, rows), lanes] = low

    f32 = dict(preferred_element_type=jnp.float32)
    both = jnp.dot(h_ref[...], m_ref[...], **f32)
    fh, fl = high_low(both[: share * total] + both[share * total :])
    if not last:
        fh_ref[...] = fh.reshape(fh_ref.shape)
        fl_ref[...] = fl.reshape(fl_ref.shape)

    def outer(a, b):
        a, b = jnp.concatenate(a, 1), jnp.concatenate(b, 1)
        return lax.dot_general(a, b, (((1,), (1,)), ((), ())), **f32)

    def part(ci, cj):
        rows_at = pl.ds(starts[ci], sizes[ci])
        lanes_at = pl.ds(blocks * starts[cj], blocks * sizes[cj])
        return (slice(None), rows_at, lanes_at), (blocks, sizes[ci], blocks * sizes[cj])

    ah = [fh[t * total : (t + 1) * total] for t in range(share)]
    al = [fl[t * total : (t + 1) * total] for t in range(share)]
    at, shape = part(c, c)
    k_ref[at] = k_ref[at] + outer(ah, ah).reshape(shape)
    cross_ref[...] = cross_ref[...] + outer(ah, al)
    for e in range(c):
        bh = [earlier[2 * e][t] for t in range(share)]
        bl = [earlier[2 * e + 1][t] for t in range(share)]
        at, shape = part(c, e)
        k_ref[at] = k_ref[at] + outer(ah + ah + al, bh + bl + bh).reshape(shape)

    @pl.when(j == pl.num_programs(0) - 1)
    def _():
        at, shape = part(c, c)
        cross = cross_ref[...]
        k_ref[at] = k_ref[at] + (cross + cross.T).reshape(shape)
        for e in range(c):
            at, _ = part(c, e)
            turned = k_ref[at].reshape(total, -1).T
            at, shape = part(e, c)
            k_ref[at] = turned.reshape(shape)


def consume(me, pieces, metric, earlier, k_so_far, n_row, nbf, starts, sizes, last):
    share, rows, aux_rows = pieces[0].shape
    total = rows * n_row
    n_aux_all = metric.shape[0]
    once = pl.Buffered(1)
    whole = pl.BlockSpec((share, rows, aux_rows), lambda j: (0, 0, 0), pipeline_mode=once)
    in_specs = [pl.BlockSpec(memory_space=pltpu.SMEM)] + [whole] * len(pieces)
    in_specs.append(pl.BlockSpec((n_aux_all, QT), lambda j: (0, j)))
    in_specs += [pl.BlockSpec((f.shape[0], f.shape[1], QT), lambda j: (0, 0, j)) for f in earlier]
    k_shape = (nbf // BS, BS, nbf)
    k_spec = pl.BlockSpec(k_shape, lambda j: (0, 0, 0), pipeline_mode=once)
    args = [me, *pieces, metric, *earlier]
    if k_so_far is not None:
        in_specs.append(k_spec)
        args.append(k_so_far)
    out_specs, out_shape = [], []
    if not last:
        out_specs += [pl.BlockSpec((share, total, QT), lambda j: (0, 0, j))] * 2
        out_shape += [jax.ShapeDtypeStruct((share, total, n_aux_all), jnp.bfloat16)] * 2
    out_specs.append(k_spec)
    out_shape.append(jax.ShapeDtypeStruct(k_shape, jnp.float32))
    scratch = [pltpu.VMEM((2 * share * total, n_aux_all), jnp.bfloat16), pltpu.VMEM((total, total), jnp.float32)]
    done = nbf // BS * sum(sizes)
    return pl.pallas_call(
        functools.partial(consume_kernel, n_row=n_row, starts=starts, sizes=sizes, last=last),
        grid=(n_aux_all // QT,),
        in_specs=in_specs,
        out_specs=out_specs,
        out_shape=out_shape,
        scratch_shapes=scratch,
        compiler_params=pltpu.CompilerParams(vmem_limit_bytes=VMEM_LIMIT),
        cost_estimate=pl.CostEstimate(
            flops=4 * share * total * n_aux_all * n_aux_all + 6 * share * total * done * n_aux_all,
            bytes_accessed=2 * metric.size + 4 * share * total * n_aux_all,
            transcendentals=0,
        ),
        name="consume",
    )(*args)


def swap_sum(parts, axis, n):
    me = lax.axis_index(axis)
    own = lax.dynamic_index_in_dim(parts, me, 0, False)
    for d in range(n - 1, 0, -1):
        given = lax.dynamic_index_in_dim(parts, me ^ d, 0, False)
        own = own + lax.ppermute(given, axis, [(s, s ^ d) for s in range(n)])
    return own


def body(integrals, pair_blocks, occupied, metric, nbf):
    n_aux, n_row, n_col = lax.axis_size("aux"), lax.axis_size("row"), lax.axis_size("col")
    occ = occupied.shape[1]
    devices = n_aux * n_row * n_col
    group = n_aux * n_row
    aux_rows, _, _ = integrals.shape
    groups = n_aux * n_col
    fits = (
        n_col == 2
        and occ % devices == 0
        and aux_rows % 128 == 0
        and group & (group - 1) == 0
        and nbf % (groups * BS) == 0
        and nbf // BS * OCT % 128 == 0
        and metric.shape[0] % QT == 0
    )
    if not fits:
        return gathered_plan(integrals, pair_blocks, occupied, metric, nbf)
    row_blocks = nbf // n_row // BS
    share = occ // devices
    me = lax.axis_index("aux") * n_row + lax.axis_index("row")
    me_array = me.reshape(1).astype(jnp.int32)

    live = (pair_blocks[0] >= 0).astype(jnp.int32)
    rows = jnp.maximum(pair_blocks[0], 0) % row_blocks
    cols = jnp.maximum(pair_blocks[1], 0) % (occupied.shape[0] // BS)
    info = jnp.concatenate([lax.axis_index("col").reshape(1).astype(jnp.int32), rows, cols, live]).astype(jnp.int32)

    sizes = tuple(e * BS // 8 for e in EIGHTHS)
    starts = tuple(sum(sizes[:c]) for c in range(len(sizes)))
    count = len(sizes)
    arrived, earlier, total = [], [], None
    order = (*range(count - 2), count - 1, count - 2)

    def use(k, me_array):
        los, ms = [tuple(v[c] for c in order[: k + 1]) for v in (starts, sizes)]
        return consume(
            me_array, arrived[order[k]], metric, earlier, total, n_row, nbf, los, ms, k == count - 1
        )

    for c in range(count):
        if c == count - 1:
            *fitted, total = use(0, me_array)
            earlier += fitted
            info, total = lax.optimization_barrier((info, total))
        other, mine = contract(info, occupied, integrals, starts[c], sizes[c], row_blocks)
        got = lax.ppermute(other, "col", [(0, 1), (1, 0)])
        shape = (group, share, row_blocks * sizes[c], aux_rows)
        pieces = list(combine(me_array, mine.reshape(shape), got.reshape(shape)))
        info, me_array, pieces[0] = lax.optimization_barrier((info, me_array, pieces[0]))
        sent = [None] * group
        for d in sorted(range(group), key=lambda d: -bin(d).count("1")):
            pairs = [(s, s ^ d) for s in range(group)]
            sent[d] = pieces[d] if d == 0 else lax.ppermute(pieces[d], ("aux", "row"), pairs)
        arrived.append(sent)

    for c in range(1, count):
        *fitted, total = use(c, me_array)
        earlier += fitted

    halves = total.reshape(n_aux, n_col, -1, nbf)
    col = lax.axis_index("col")
    given = lax.dynamic_index_in_dim(halves, 1 - col, 1, False)
    part = lax.dynamic_index_in_dim(halves, col, 1, False) + lax.ppermute(given, "col", [(0, 1), (1, 0)])
    part = swap_sum(part, "aux", n_aux)
    blocks = nbf // BS
    part = part.T
    strips = [part[blocks * lo : blocks * (lo + m)].reshape(blocks, m, -1) for lo, m in zip(starts, sizes)]
    part = jnp.concatenate(strips, 1).reshape(n_row, nbf // n_row, -1)
    return swap_sum(part, "row", n_row)


def solution(mesh):
    def local(*args, nbf):
        return body(*args, nbf)

    def whole(integrals, pair_blocks, occupied, metric):
        nbf = occupied.shape[0]
        return jax.shard_map(
            functools.partial(local, nbf=nbf),
            mesh=mesh,
            in_specs=(P("aux", ("row", "col"), None), P(None, ("row", "col")), P("col", None), P()),
            out_specs=P("row", ("aux", "col")),
            check_vma=False,
        )(integrals, pair_blocks, occupied, metric)

    return whole
```
